32 devices in a mesh: groups: 2 (over y), row: 4 (over z), col: 4 (over x, core).
Axes of the slice: x: 2, y: 2, z: 4, core: 2. Of those that a mesh axis runs over, the one named last changes fastest.
Arguments:
- pair: bfloat16 [512, 16384], P(('groups', 'row'), 'col'), parts along dimension 0, may hold values from -6 to 6
- res_mask: int32 [512], P('groups'), parts along dimension 0, may hold values 0 or 1
- present: int32 [512], P('groups'), parts along dimension 0, may hold values 0 or 1
- ln_in_gain: float32 [64], replicated, may hold values from 0.1 to 1.9
- w_proj: bfloat16 [64, 256], replicated, may hold values from -0.75 to 0.75
- w_gate: bfloat16 [64, 64], replicated, may hold values from -0.75 to 0.75
- ln_out_gain: float32 [64], replicated, may hold values from 0.1 to 1.9
- w_out: bfloat16 [64, 64], replicated, may hold values from -0.75 to 0.75
Outputs:
- update: bfloat16 [512, 16384], P(('groups', 'row'), 'col'), parts along dimension 0
The draws below stay inside these ranges and needn't reach their ends.
There are 2 independent parts, one for each index of `groups`. The reference program is written for one: setup_inputs(seed, part) draws one part's arguments, and reference() takes and returns one part's arrays. A program takes and returns all parts, laid end to end along the dimension named above; an argument that names none is the same for every part. Nothing has to cross between parts.
All inputs are finite; a program needn't handle non-finite values.
Results may differ from the reference program's by a relative error of at most 0.0078.
Values may be sent and summed in bfloat16 or wider, within the bound.
A program may use at most 64 MiB of HBM per device.

```python
import jax
import jax.numpy as jnp
from jax import lax

CP = 64
HID = 64
N = 256


def set_ends(array, stream_key, low, high):
    extent = array.shape
    spot = [jax.random.randint(jax.random.fold_in(stream_key, axis), (), 0, extent[axis]) for axis in range(len(extent))]
    array = array.at[tuple(spot)].set(low)
    longest = extent.index(max(extent))
    spot[longest] = (spot[longest] + 1) % extent[longest]
    return array.at[tuple(spot)].set(high)


def block_levels(own_key, shape, pieces, smallest, largest):
    def one(position, blocks):
        steps = jax.random.uniform(jax.random.fold_in(jax.random.fold_in(own_key, 6), position), (blocks,), jnp.float32, smallest / len(pieces), largest / len(pieces))
        return jnp.repeat(jnp.exp(steps), shape[position] // blocks).reshape((-1,) + (1,) * (len(shape) - position - 1))

    level = one(*pieces[0])
    for cut in pieces[1:]:
        level = level * one(*cut)
    return level


def noise(stream_key, shape, width, limit, cuts=(), held_as=jnp.bfloat16):
    drawn = jax.random.normal(stream_key, shape, jnp.float32) * width
    if len(cuts) > 0:
        drawn = block_levels(stream_key, shape, cuts, -0.22, 0.18) * drawn
    return jnp.clip(drawn, min=-limit, max=limit).astype(held_as)


def setup_inputs(seed: int = 0, part: int = 0) -> dict:
    keys = jax.random.split(jax.random.key(seed), 9)
    part_splits = jax.random.split(jax.random.fold_in(keys[8], part), 9)
    pair = noise(part_splits[0], (N, N * CP), 1.0, 6.0, ((0, 4), (1, 4)))
    res_mask = set_ends((jax.random.randint(part_splits[1], (N,), 0, 8) < 7).astype(jnp.int32), jax.random.fold_in(part_splits[1], 1), 0, 1)
    present = set_ends((jax.random.randint(part_splits[2], (N,), 0, 4) < 3).astype(jnp.int32), jax.random.fold_in(part_splits[2], 1), 0, 1)
    ln_in_gain = jnp.clip(1.0 + 0.18 * jax.random.normal(keys[3], (CP,), jnp.float32), 0.1, 1.9)
    w_proj = noise(keys[4], (CP, 4 * HID), CP ** -0.5, 0.75)
    w_gate = noise(keys[5], (CP, CP), CP ** -0.5, 0.75)
    ln_out_gain = jnp.clip(1.0 + 0.18 * jax.random.normal(keys[6], (HID,), jnp.float32), 0.1, 1.9)
    w_out = noise(keys[7], (HID, CP), HID ** -0.5, 0.75)
    return {"pair": pair, "res_mask": res_mask, "present": present, "ln_in_gain": ln_in_gain, "w_proj": w_proj, "w_gate": w_gate, "ln_out_gain": ln_out_gain, "w_out": w_out}


def layer_norm(values, gain):
    mean = lax.optimization_barrier(jnp.mean(values, axis=-1, keepdims=True))
    var = lax.optimization_barrier(jnp.mean((values - mean) ** 2, axis=-1, keepdims=True))
    return (values - mean) * lax.rsqrt(var + 1e-05) * gain

def reference(pair, res_mask, present, ln_in_gain, w_proj, w_gate, ln_out_gain, w_out):
    z = pair.astype(jnp.float32).reshape(N, N, CP)
    normed = layer_norm(z, ln_in_gain).astype(jnp.bfloat16).reshape(N * N, CP)
    proj = jnp.dot(normed, w_proj, preferred_element_type=jnp.float32).reshape(N, N, 4 * HID)
    weight = (res_mask * present).astype(jnp.float32)
    pair_mask = (weight[:, None] * weight[None, :])[:, :, None]
    a_val = (pair_mask * jax.nn.sigmoid(proj[:, :, :HID]) * proj[:, :, HID:2 * HID]).astype(jnp.bfloat16)
    b_val = (pair_mask * jax.nn.sigmoid(proj[:, :, 2 * HID:3 * HID]) * proj[:, :, 3 * HID:]).astype(jnp.bfloat16)
    gate = jax.nn.sigmoid(jnp.dot(normed, w_gate, preferred_element_type=jnp.float32)).reshape(N, N, CP)
    tri = jnp.einsum('kic,kjc->ijc', a_val.astype(jnp.float32), b_val.astype(jnp.float32), precision=lax.Precision.HIGHEST)
    tri_norm = layer_norm(tri, ln_out_gain).astype(jnp.bfloat16).reshape(N * N, HID)
    projected = jnp.dot(tri_norm, w_out, preferred_element_type=jnp.float32).reshape(N, N, CP)
    return (gate * projected).astype(jnp.bfloat16).reshape(N, N * CP)
```

```python
import functools

import jax
import jax.numpy as jnp
from jax import lax
from jax.experimental import pallas as pl
from jax.experimental.pallas import tpu as pltpu
from jax.sharding import PartitionSpec as P

NT = (((1,), (1,)), ((), ()))
NN = (((1,), (0,)), ((), ()))
EIGHT = 8
LANES = 128
CHUNKS = 4


def dot(lhs, rhs, dims):
    return lax.dot_general(lhs, rhs, dims, preferred_element_type=jnp.float32)


def flipped(value, mask, count):
    total = 0
    step = 1
    while step < count:
        total = total + ((value // step + mask // step) % 2) * step
        step *= 2
    return total


def lane_pair(left, right, half):
    w = LANES // 2
    return jnp.concatenate(
        [left[:, half * w : (half + 1) * w], right[:, half * w : (half + 1) * w]], axis=1
    )


def iota(shape, dim):
    return lax.broadcasted_iota(jnp.int32, shape, dim)


def fused_kernel(
    R, C, pair_hbm, res_hbm, present_hbm, gain_in_hbm, w_proj_hbm, w_gate_hbm, gain_out_hbm,
    w_out_hbm, out_hbm, pair_ref, res_ref, present_ref, gain_in_ref, w_proj_ref, w_gate_ref,
    gain_out_ref, w_out_ref, out_ref, normed, gate, wide, masks, send1, recv1, send2, recv2,
    send_sem1, recv_sem1, send_sem2, recv_sem2, in_sem, out_sem,
):
    f32, bf16 = jnp.float32, jnp.bfloat16
    rows = pair_ref.shape[0]
    chans = w_gate_ref.shape[0]
    hidden = w_out_ref.shape[0]
    ndev = R * C
    depth = R // 2
    team = depth * C
    own = hidden // team
    per = own // CHUNKS
    groups = normed.shape[0] // rows
    pairs = groups // 2
    block = EIGHT * chans
    half_block = block // 2
    r, c = lax.axis_index("row"), lax.axis_index("col")
    me = r * C + c
    half_row = r // depth * depth
    seat = r % depth * C + c

    def mate(n):
        row = half_row + flipped(r % depth, depth - 1 - n // C, depth)
        return row, flipped(c, C - 1 - n % C, C)

    def partner(n):
        return flipped(r, R - 1 - n // C, R), flipped(c, C - 1 - n % C, C)

    barrier = pltpu.get_barrier_semaphore()

    def greet(n, carry):
        pr, pc = partner(n)
        pl.semaphore_signal(
            barrier, inc=1, device_id={"row": pr, "col": pc}, device_id_type=pl.DeviceIdType.MESH
        )
        return carry

    lax.fori_loop(0, ndev - 1, greet, 0)
    loads = [
        pltpu.make_async_copy(source, target, in_sem.at[at])
        for at, (source, target) in enumerate(
            (
                (pair_hbm, pair_ref), (gain_in_hbm, gain_in_ref), (gain_out_hbm, gain_out_ref),
                (res_hbm, res_ref), (present_hbm, present_ref), (w_proj_hbm, w_proj_ref),
                (w_gate_hbm, w_gate_ref), (w_out_hbm, w_out_ref),
            )
        )
    ]
    for load in loads:
        load.start()
    for load in loads:
        load.wait()

    eye = iota((chans, chans), 0) == iota((chans, chans), 1)
    sub_id, lane_in = iota((chans, block), 0), iota((chans, block), 1)

    def over_lanes(gain_ref, match):
        column = jnp.sum(jnp.where(eye, gain_ref[...], 0.0), axis=1, keepdims=True)
        return jnp.sum(jnp.where(match, column, 0.0), axis=0, keepdims=True)

    gain_in = over_lanes(gain_in_ref, lane_in % chans == sub_id)
    gain_out = over_lanes(gain_out_ref, lane_in // EIGHT == sub_id)

    same = (iota((half_block, half_block), 0) // chans) == (
        iota((half_block, half_block), 1) // chans
    )
    ones = same.astype(f32).astype(bf16)
    for h in range(2):
        parts = []
        for qp in range(pairs):
            for par in range(2):
                lo = (par * pairs + qp) * block + h * half_block
                parts.append(pair_ref[:, lo : lo + half_block])
        x = jnp.concatenate(parts, axis=0)
        d = x.astype(f32) - dot(x, ones, NN) * (1.0 / chans)
        sq = d * d
        hi = sq.astype(bf16)
        lo_part = (sq - hi.astype(f32)).astype(bf16)
        var = (dot(hi, ones, NN) + dot(lo_part, ones, NN)) * (1.0 / chans)
        y = d * lax.rsqrt(var + 1e-05) * gain_in[:, h * half_block : (h + 1) * half_block]
        normed[:, h * half_block : (h + 1) * half_block] = y.astype(bf16)

    count = res_ref.shape[1]
    alive = (res_ref[...] * present_ref[...]).astype(f32)
    wide_lanes = groups * rows
    res_id, lane = iota((count, wide_lanes), 0), iota((count, wide_lanes), 1)
    group = (lane // rows) % 2 * pairs + lane // LANES
    is_row = (res_id == r * rows + lane % rows).astype(f32).astype(bf16)
    is_col = (res_id // EIGHT == c * groups + group).astype(f32).astype(bf16)
    shape = (per * EIGHT, count)
    phase = iota(shape, 0) % EIGHT == iota(shape, 1) % EIGHT
    rows_alive = dot(jnp.broadcast_to(alive, shape).astype(bf16), is_row, NN)
    masks[...] = rows_alive * dot(jnp.where(phase, alive, 0.0).astype(bf16), is_col, NN)

    stacked = jnp.concatenate([w_proj_ref[...]] * EIGHT, axis=0)
    part = per * EIGHT
    n_rows = team * 4 * part
    out_chans = w_proj_ref.shape[1]
    diag = (iota((n_rows, block), 0) % EIGHT) == (iota((n_rows, block), 1) // chans)
    row_id = iota((n_rows, out_chans), 0)
    target = row_id // part % 4 * hidden + row_id // (4 * part) * own + row_id % part // EIGHT
    target = iota((n_rows, out_chans), 1) - target

    def project(h):
        pick = (target == h * per).astype(f32).astype(bf16)
        weights = jnp.where(diag, dot(pick, stacked, NT), 0.0).astype(bf16)
        res = dot(weights, normed[...], NT)
        mask = masks[...]
        for dest in range(team):
            for which in range(2):
                lo = (4 * dest + 2 * which) * part
                g, v = res[lo : lo + part], res[lo + part : lo + 2 * part]
                val = mask * jax.nn.sigmoid(g) * v
                for ch in range(per):
                    tile = jnp.concatenate(
                        [
                            val[ch * EIGHT : (ch + 1) * EIGHT, qp * LANES : (qp + 1) * LANES]
                            for qp in range(pairs)
                        ],
                        axis=0,
                    )
                    send1[h, dest, ch, which] = tile.astype(bf16)

    def remote(source, target, ssem, rsem, where):
        return pltpu.make_async_remote_copy(
            src_ref=source, dst_ref=target, send_sem=ssem, recv_sem=rsem,
            device_id={"row": where[0], "col": where[1]}, device_id_type=pl.DeviceIdType.MESH,
        )

    def copy1(h, n, sending):
        where = mate(n)
        p = (where[0] - half_row) * C + where[1]
        at = seat if sending else p
        return remote(
            send1.at[h, p], recv1.at[h, at], send_sem1.at[0], recv_sem1.at[h], where
        )

    def copy2(piece, n, sending):
        where = partner(n)
        p = where[0] * C + where[1]
        at = me if sending else p
        last = CHUNKS - 1
        key = (lambda d: (piece, d)) if piece < last else (lambda d: (last, d, piece - last))
        return remote(
            send2.at[key(p)], recv2.at[key(at)],
            send_sem2.at[0], recv_sem2.at[piece], where,
        )

    def each(total, body):
        def run(n, carry):
            body(n)
            return carry

        lax.fori_loop(0, total - 1, run, 0)

    gate_rows = jnp.concatenate([w_gate_ref[...]] * (half_block // chans), axis=0)
    spread = ((iota((chans, block), 1) % chans) == iota((chans, block), 0)).astype(f32).astype(bf16)
    w_gate4 = jnp.where(same, dot(gate_rows, spread[:, :half_block], NN), 0.0).astype(bf16)

    def output_gate(h):
        cols = slice(h * half_block, (h + 1) * half_block)
        gate[:, cols] = jax.nn.sigmoid(dot(normed[:, cols], w_gate4, NN))

    own1 = [
        pltpu.make_async_copy(send1.at[h, seat], recv1.at[h, seat], recv_sem1.at[h])
        for h in range(CHUNKS)
    ]

    def landed(ref, sem):
        pltpu.make_async_copy(ref, ref, sem).wait()

    tiled = dot(w_out_ref[...], spread, NN).astype(bf16)
    big = hidden * EIGHT
    pick_out = ((iota((big, hidden), 0) // EIGHT) == iota((big, hidden), 1)).astype(f32).astype(bf16)
    diag_out = (iota((big, block), 0) % EIGHT) == (iota((big, block), 1) // chans)

    sub = pairs * EIGHT

    def multiply(h, ch):
        full = []
        for which in range(2):
            by_parity = [[], []]
            for rp in range(depth // 2):
                one, two = (
                    jnp.concatenate(
                        [recv1[h, (2 * rp + e) * C + cc, ch, which] for cc in range(C)], axis=0
                    ).astype(f32)
                    for e in range(2)
                )
                for par in range(2):
                    by_parity[par].append(lane_pair(one, two, par).astype(bf16))
            full.append([jnp.concatenate(p, axis=1) for p in by_parity])
        a_rows = jnp.concatenate(
            [full[0][par][cc * sub : (cc + 1) * sub] for cc in range(C) for par in range(2)], axis=0
        )
        even, odd = (dot(full[1][par], a_rows, NT) for par in range(2))
        for rp in range(R // 2):
            cols = slice(rp * LANES, (rp + 1) * LANES)
            for e in range(2):
                tile = lane_pair(even[:, cols], odd[:, cols], e).astype(bf16)
                for cc in range(C):
                    for two in range(2):
                        lo = cc * sub + two * (sub // 2)
                        send2[h, (2 * rp + e) * C + cc, two, ch] = tile[lo : lo + sub // 2]

    def own2(piece):
        if piece < CHUNKS - 1:
            source, target = send2.at[piece, me], recv2.at[piece, me]
        else:
            half = piece - CHUNKS + 1
            source, target = send2.at[CHUNKS - 1, me, half], recv2.at[CHUNKS - 1, me, half]
        return pltpu.make_async_copy(source, target, recv_sem2.at[piece])

    def answer(h):
        landed(recv1.at[h], recv_sem1.at[h])
        for ch in range(per):
            multiply(h, ch)
        for piece in (h,) if h < CHUNKS - 1 else (h, h + 1):
            each(ndev, lambda n, piece=piece: copy2(piece, n, True).start())
            own2(piece).start()

    for h in range(CHUNKS):
        project(h)
        if h == 0:
            pl.semaphore_wait(barrier, ndev - 1)
        if h in (1, 2):
            output_gate(h - 1)
        each(team, lambda n, h=h: copy1(h, n, True).start())
        own1[h].start()
        if h >= 2:
            answer(h - 2)
    for h in range(max(CHUNKS - 2, 0), CHUNKS):
        answer(h)
    for h in range(max(CHUNKS, 1), 3):
        output_gate(h - 1)
    wide[...] = jnp.where(diag_out, dot(pick_out, tiled, NN), 0.0).astype(bf16)

    for piece in range(CHUNKS - 1):
        landed(recv2.at[piece], recv_sem2.at[piece])
    for two in range(pairs // 2):
        landed(recv2.at[CHUNKS - 1, :, two], recv_sem2.at[CHUNKS - 1 + two])
        t = jnp.concatenate(
            [
                (recv2[h, :team, two].astype(f32) + recv2[h, team:, two].astype(f32))[:, None]
                for h in range(CHUNKS)
            ],
            axis=1,
        ).reshape(hidden, 16, LANES)
        mean = jnp.sum(t, axis=0, keepdims=True) * (1.0 / hidden)
        d = t - mean
        var = jnp.sum(d * d, axis=0, keepdims=True) * (1.0 / hidden)
        y = d * lax.rsqrt(var + 1e-05)
        for e in range(2):
            qp = 2 * two + e
            flat = y[:, e * EIGHT : (e + 1) * EIGHT, :].reshape(big, LANES)
            lhs = (flat.T * gain_out).astype(bf16)
            res = dot(lhs, wide[...], NN)
            for par in range(2):
                g = gate[(2 * qp + par) * rows : (2 * qp + par + 1) * rows, :]
                val = g * res[par * rows : (par + 1) * rows]
                lo = (par * pairs + qp) * block
                out_ref[:, lo : lo + block] = val.astype(bf16)
                pltpu.make_async_copy(
                    out_ref.at[:, pl.ds(lo, block)], out_hbm.at[:, pl.ds(lo, block)], out_sem
                ).start()
    landed(out_ref, out_sem)
    landed(send1.at[:, pl.ds(0, team - 1)], send_sem1.at[0])
    landed(send2.at[:, pl.ds(0, ndev - 1)], send_sem2.at[0])


def fused(pair, res_mask, present, ln_in_gain, w_proj, w_gate, ln_out_gain, w_out):
    R, C = lax.axis_size("row"), lax.axis_size("col")
    rows, width = pair.shape
    chans, hidden = w_gate.shape[0], w_out.shape[0]
    cols = width // chans
    groups = cols // EIGHT
    pairs = groups // 2
    ndev = R * C
    team = ndev // 2
    own = hidden // team
    per = own // CHUNKS
    bf16 = jnp.bfloat16
    anywhere = pl.BlockSpec(memory_space=pl.ANY)
    operands = (
        pair, res_mask[None, :], present[None, :], ln_in_gain[None, :], w_proj, w_gate,
        ln_out_gain[None, :], w_out,
    )
    sub = pairs * EIGHT
    return pl.pallas_call(
        functools.partial(fused_kernel, R, C),
        out_shape=jax.ShapeDtypeStruct(pair.shape, bf16),
        in_specs=[anywhere] * len(operands),
        out_specs=anywhere,
        scratch_shapes=[pltpu.VMEM(value.shape, value.dtype) for value in operands]
        + [
            pltpu.VMEM(pair.shape, bf16),
            pltpu.VMEM((groups * rows, EIGHT * chans), bf16),
            pltpu.VMEM((groups * rows, EIGHT * chans), jnp.float32),
            pltpu.VMEM((hidden * EIGHT, EIGHT * chans), bf16),
            pltpu.VMEM((per * EIGHT, groups * rows), jnp.float32),
            pltpu.VMEM((CHUNKS, team, per, 2, sub, LANES), bf16),
            pltpu.VMEM((CHUNKS, team, per, 2, sub, LANES), bf16),
            pltpu.VMEM((CHUNKS, ndev, 2, per, sub // 2, LANES), bf16),
            pltpu.VMEM((CHUNKS, ndev, 2, per, sub // 2, LANES), bf16),
            pltpu.SemaphoreType.DMA((1,)),
            pltpu.SemaphoreType.DMA((CHUNKS,)),
            pltpu.SemaphoreType.DMA((1,)),
            pltpu.SemaphoreType.DMA((CHUNKS + 1,)),
            pltpu.SemaphoreType.DMA((len(operands),)),
            pltpu.SemaphoreType.DMA,
        ],
        compiler_params=pltpu.CompilerParams(collective_id=0, has_side_effects=True),
    )(*operands)


def fits(R, C, rows, cols, chans, hidden):
    powers = all(n & (n - 1) == 0 for n in (R, C))
    return (
        powers
        and R == C
        and R % 4 == 0
        and rows == cols == LANES // 2
        and chans == hidden == LANES // 2
        and hidden % (R * C // 2 * CHUNKS) == 0
    )


def swapped(value, axis, bit):
    mask = 2**bit
    pairs = [(source, source ^ mask) for source in range(lax.axis_size(axis))]
    return lax.ppermute(value, axis, pairs)


def layer_norm(values, gain):
    mean = jnp.mean(values, axis=-1, keepdims=True)
    var = jnp.mean((values - mean) ** 2, axis=-1, keepdims=True)
    return (values - mean) * lax.rsqrt(var + 1e-05) * gain


def local(pair, res_mask, present, ln_in_gain, w_proj, w_gate, ln_out_gain, w_out):
    rows_here, width = pair.shape
    chans = w_gate.shape[0]
    hidden = w_out.shape[0]
    cols_here = width // chans
    row_count = lax.axis_size("row")
    col_count = lax.axis_size("col")
    if fits(row_count, col_count, rows_here, cols_here, chans, hidden):
        return fused(pair, res_mask, present, ln_in_gain, w_proj, w_gate, ln_out_gain, w_out)
    row_index = lax.axis_index("row")
    col_index = lax.axis_index("col")
    z_tile = pair.astype(jnp.float32).reshape(rows_here, cols_here, chans)
    normed = (
        layer_norm(z_tile, ln_in_gain).astype(jnp.bfloat16).reshape(rows_here * cols_here, chans)
    )
    proj = jnp.dot(normed, w_proj, preferred_element_type=jnp.float32).reshape(
        rows_here, cols_here, 4 * hidden
    )
    weight = (res_mask * present).astype(jnp.float32)
    weight_rows = lax.dynamic_slice_in_dim(weight, row_index * rows_here, rows_here)
    weight_cols = lax.dynamic_slice_in_dim(weight, col_index * cols_here, cols_here)
    pair_mask = (weight_rows[:, None] * weight_cols[None, :])[:, :, None]
    a_tile = (
        pair_mask * jax.nn.sigmoid(proj[:, :, :hidden]) * proj[:, :, hidden : 2 * hidden]
    ).astype(jnp.bfloat16)
    b_tile = (
        pair_mask * jax.nn.sigmoid(proj[:, :, 2 * hidden : 3 * hidden]) * proj[:, :, 3 * hidden :]
    ).astype(jnp.bfloat16)
    gate = jax.nn.sigmoid(jnp.dot(normed, w_gate, preferred_element_type=jnp.float32)).reshape(
        rows_here, cols_here, chans
    )
    factor = 2 if row_count == 4 * col_count else 1
    square_rows = factor * rows_here
    wide_rows = lax.all_gather(a_tile, "col", axis=1, tiled=True)
    spread = wide_rows.reshape(rows_here, row_count // factor, 1, square_rows, hidden)
    spread = jnp.repeat(spread, factor, axis=2).reshape(rows_here, row_count * square_rows, hidden)
    a_square = lax.all_to_all(spread, "row", split_axis=1, concat_axis=0, tiled=True)
    copies = jnp.tile(b_tile, (1, row_count // factor, 1))
    b_square = lax.all_to_all(copies, "row", split_axis=1, concat_axis=0, tiled=True)
    tri_square = jnp.einsum("kic,kjc->ijc", a_square, b_square, preferred_element_type=jnp.float32)
    normed_square = layer_norm(tri_square, ln_out_gain).astype(jnp.bfloat16)
    if factor == 1:
        tri_norm = normed_square
    else:
        parity = row_index % 2
        own_part = lax.dynamic_slice_in_dim(normed_square, parity * rows_here, rows_here, 0)
        other_part = lax.dynamic_slice_in_dim(normed_square, (1 - parity) * rows_here, rows_here, 0)
        received = swapped(other_part, "row", 0)
        tri_norm = jnp.where(
            parity == 0,
            jnp.concatenate([own_part, received], axis=1),
            jnp.concatenate([received, own_part], axis=1),
        )
    flat_norm = tri_norm.reshape(rows_here * cols_here, hidden)
    projected = jnp.dot(flat_norm, w_out, preferred_element_type=jnp.float32).reshape(
        rows_here, cols_here, chans
    )
    return (gate * projected).astype(jnp.bfloat16).reshape(rows_here, cols_here * chans)


def solution(mesh):
    in_specs = (P(("groups", "row"), "col"), P("groups"), P("groups"), P(), P(), P(), P(), P())
    out_specs = P(("groups", "row"), "col")
    return jax.shard_map(local, mesh=mesh, in_specs=in_specs, out_specs=out_specs, check_vma=False)
```

```python
import functools

import jax
import jax.numpy as jnp
from jax import lax
from jax.experimental import pallas as pl
from jax.experimental.pallas import tpu as pltpu
from jax.sharding import PartitionSpec as P

NT = (((1,), (1,)), ((), ()))
NN = (((1,), (0,)), ((), ()))
EIGHT = 8
LANES = 128
CHUNKS = 4
WRITE_GRANT = 2**20


def dot(lhs, rhs, dims):
    return lax.dot_general(lhs, rhs, dims, preferred_element_type=jnp.float32)


def flipped(value, mask, count):
    total = 0
    step = 1
    while step < count:
        total = total + ((value // step + mask // step) % 2) * step
        step *= 2
    return total


def lane_pair(left, right, half):
    w = LANES // 2
    return jnp.concatenate(
        [left[:, half * w : (half + 1) * w], right[:, half * w : (half + 1) * w]], axis=1
    )


def iota(shape, dim):
    return lax.broadcasted_iota(jnp.int32, shape, dim)


def fused_kernel(
    R, C, pair_hbm, res_hbm, present_hbm, gain_in_hbm, w_proj_hbm, w_gate_hbm, gain_out_hbm,
    w_out_hbm, out_ref, pair_ref, res_ref, present_ref, gain_in_ref, w_proj_ref, w_gate_ref,
    gain_out_ref, w_out_ref, normed, gate, wide, masks, send1, recv1, send2, recv2,
    send_sem1, recv_sem1, send_sem2, recv_sem2, in_sem,
):
    f32, bf16 = jnp.float32, jnp.bfloat16
    rows = pair_ref.shape[0]
    chans = w_gate_ref.shape[0]
    hidden = w_out_ref.shape[0]
    ndev = R * C
    depth = R // 2
    team = depth * C
    own = hidden // team
    per = own // CHUNKS
    groups = normed.shape[0] // rows
    pairs = groups // 2
    block = EIGHT * chans
    half_block = block // 2
    r, c = lax.axis_index("row"), lax.axis_index("col")
    me = r * C + c
    half_row = r // depth * depth
    seat = r % depth * C + c

    def mate(n):
        row = half_row + flipped(r % depth, depth - 1 - n // C, depth)
        return row, flipped(c, C - 1 - n % C, C)

    def partner(n):
        return flipped(r, R - 1 - n // C, R), flipped(c, C - 1 - n % C, C)

    barrier = pltpu.get_barrier_semaphore()

    def greet(n, carry):
        pr, pc = partner(n)
        pl.semaphore_signal(
            barrier, inc=1, device_id={"row": pr, "col": pc}, device_id_type=pl.DeviceIdType.MESH
        )
        return carry

    lax.fori_loop(0, ndev - 1, greet, 0)
    loads = [
        pltpu.make_async_copy(source, target, in_sem.at[at])
        for at, (source, target) in enumerate(
            (
                (pair_hbm, pair_ref), (gain_in_hbm, gain_in_ref), (gain_out_hbm, gain_out_ref),
                (res_hbm, res_ref), (present_hbm, present_ref), (w_proj_hbm, w_proj_ref),
                (w_gate_hbm, w_gate_ref), (w_out_hbm, w_out_ref),
            )
        )
    ]
    for load in loads:
        load.start()
    for load in loads:
        load.wait()

    eye = iota((chans, chans), 0) == iota((chans, chans), 1)
    sub_id, lane_in = iota((chans, block), 0), iota((chans, block), 1)

    def over_lanes(gain_ref, match):
        column = jnp.sum(jnp.where(eye, gain_ref[...], 0.0), axis=1, keepdims=True)
        return jnp.sum(jnp.where(match, column, 0.0), axis=0, keepdims=True)

    gain_in = over_lanes(gain_in_ref, lane_in % chans == sub_id)
    gain_out = over_lanes(gain_out_ref, lane_in // EIGHT == sub_id)

    same = (iota((half_block, half_block), 0) // chans) == (
        iota((half_block, half_block), 1) // chans
    )
    ones = same.astype(f32).astype(bf16)
    for h in range(2):
        parts = []
        for qp in range(pairs):
            for par in range(2):
                lo = (par * pairs + qp) * block + h * half_block
                parts.append(pair_ref[:, lo : lo + half_block])
        x = jnp.concatenate(parts, axis=0)
        d = x.astype(f32) - dot(x, ones, NN) * (1.0 / chans)
        sq = d * d
        hi = sq.astype(bf16)
        lo_part = (sq - hi.astype(f32)).astype(bf16)
        var = (dot(hi, ones, NN) + dot(lo_part, ones, NN)) * (1.0 / chans)
        y = d * lax.rsqrt(var + 1e-05) * gain_in[:, h * half_block : (h + 1) * half_block]
        normed[:, h * half_block : (h + 1) * half_block] = y.astype(bf16)

    count = res_ref.shape[1]
    alive = (res_ref[...] * present_ref[...]).astype(f32)
    wide_lanes = groups * rows
    res_id, lane = iota((count, wide_lanes), 0), iota((count, wide_lanes), 1)
    group = (lane // rows) % 2 * pairs + lane // LANES
    is_row = (res_id == r * rows + lane % rows).astype(f32).astype(bf16)
    is_col = (res_id // EIGHT == c * groups + group).astype(f32).astype(bf16)
    shape = (per * EIGHT, count)
    phase = iota(shape, 0) % EIGHT == iota(shape, 1) % EIGHT
    rows_alive = dot(jnp.broadcast_to(alive, shape).astype(bf16), is_row, NN)
    masks[...] = rows_alive * dot(jnp.where(phase, alive, 0.0).astype(bf16), is_col, NN)

    stacked = jnp.concatenate([w_proj_ref[...]] * EIGHT, axis=0)
    part = per * EIGHT
    n_rows = team * 4 * part
    out_chans = w_proj_ref.shape[1]
    diag = (iota((n_rows, block), 0) % EIGHT) == (iota((n_rows, block), 1) // chans)
    row_id = iota((n_rows, out_chans), 0)
    target = row_id // part % 4 * hidden + row_id // (4 * part) * own + row_id % part // EIGHT
    target = iota((n_rows, out_chans), 1) - target

    def project(h):
        pick = (target == h * per).astype(f32).astype(bf16)
        weights = jnp.where(diag, dot(pick, stacked, NT), 0.0).astype(bf16)
        res = dot(weights, normed[...], NT)
        mask = masks[...]
        for dest in range(team):
            for which in range(2):
                lo = (4 * dest + 2 * which) * part
                g, v = res[lo : lo + part], res[lo + part : lo + 2 * part]
                val = mask * jax.nn.sigmoid(g) * v
                for ch in range(per):
                    tile = jnp.concatenate(
                        [
                            val[ch * EIGHT : (ch + 1) * EIGHT, qp * LANES : (qp + 1) * LANES]
                            for qp in range(pairs)
                        ],
                        axis=0,
                    )
                    send1[h, dest, ch, which] = tile.astype(bf16)

    def remote(source, target, ssem, rsem, where):
        return pltpu.make_async_remote_copy(
            src_ref=source, dst_ref=target, send_sem=ssem, recv_sem=rsem,
            device_id={"row": where[0], "col": where[1]}, device_id_type=pl.DeviceIdType.MESH,
        )

    def copy1(h, n, sending):
        where = mate(n)
        p = (where[0] - half_row) * C + where[1]
        at = seat if sending else p
        return remote(
            send1.at[h, p], recv1.at[h, at], send_sem1.at[0], recv_sem1.at[h], where
        )

    def copy2(piece, n, sending):
        where = partner(n)
        p = where[0] * C + where[1]
        at = me if sending else p
        last = CHUNKS - 1
        key = (lambda d: (piece, d)) if piece < last else (lambda d: (last, d, piece - last))
        return remote(
            send2.at[key(p)], recv2.at[key(at)],
            send_sem2.at[0], recv_sem2.at[piece], where,
        )

    def each(total, body):
        def run(n, carry):
            body(n)
            return carry

        lax.fori_loop(0, total - 1, run, 0)

    gate_rows = jnp.concatenate([w_gate_ref[...]] * (half_block // chans), axis=0)
    spread = ((iota((chans, block), 1) % chans) == iota((chans, block), 0)).astype(f32).astype(bf16)
    w_gate4 = jnp.where(same, dot(gate_rows, spread[:, :half_block], NN), 0.0).astype(bf16)

    def output_gate(h):
        cols = slice(h * half_block, (h + 1) * half_block)
        gate[:, cols] = jax.nn.sigmoid(dot(normed[:, cols], w_gate4, NN))

    own1 = [
        pltpu.make_async_copy(send1.at[h, seat], recv1.at[h, seat], recv_sem1.at[h])
        for h in range(CHUNKS)
    ]

    def landed(ref, sem):
        pltpu.make_async_copy(ref, ref, sem).wait()

    tiled = dot(w_out_ref[...], spread, NN).astype(bf16)
    big = hidden * EIGHT
    pick_out = ((iota((big, hidden), 0) // EIGHT) == iota((big, hidden), 1)).astype(f32).astype(bf16)
    diag_out = (iota((big, block), 0) % EIGHT) == (iota((big, block), 1) // chans)

    sub = pairs * EIGHT

    def multiply(h, ch):
        full = []
        for which in range(2):
            by_parity = [[], []]
            for rp in range(depth // 2):
                one, two = (
                    jnp.concatenate(
                        [recv1[h, (2 * rp + e) * C + cc, ch, which] for cc in range(C)], axis=0
                    ).astype(f32)
                    for e in range(2)
                )
                for par in range(2):
                    by_parity[par].append(lane_pair(one, two, par).astype(bf16))
            full.append([jnp.concatenate(p, axis=1) for p in by_parity])
        a_rows = jnp.concatenate(
            [full[0][par][cc * sub : (cc + 1) * sub] for cc in range(C) for par in range(2)], axis=0
        )
        even, odd = (dot(full[1][par], a_rows, NT) for par in range(2))
        for rp in range(R // 2):
            cols = slice(rp * LANES, (rp + 1) * LANES)
            for e in range(2):
                tile = lane_pair(even[:, cols], odd[:, cols], e).astype(bf16)
                for cc in range(C):
                    for two in range(2):
                        lo = cc * sub + two * (sub // 2)
                        send2[h, (2 * rp + e) * C + cc, two, ch] = tile[lo : lo + sub // 2]

    def own2(piece):
        if piece < CHUNKS - 1:
            source, target = send2.at[piece, me], recv2.at[piece, me]
        else:
            half = piece - CHUNKS + 1
            source, target = send2.at[CHUNKS - 1, me, half], recv2.at[CHUNKS - 1, me, half]
        return pltpu.make_async_copy(source, target, recv_sem2.at[piece])

    def answer(h):
        landed(recv1.at[h], recv_sem1.at[h])
        for ch in range(per):
            multiply(h, ch)
        for piece in (h,) if h < CHUNKS - 1 else (h, h + 1):
            each(ndev, lambda n, piece=piece: copy2(piece, n, True).start())
            own2(piece).start()

    for h in range(CHUNKS):
        project(h)
        if h == 0:
            pl.semaphore_wait(barrier, ndev - 1)
        if h in (1, 2):
            output_gate(h - 1)
        each(team, lambda n, h=h: copy1(h, n, True).start())
        own1[h].start()
        if h >= 2:
            answer(h - 2)
    for h in range(max(CHUNKS - 2, 0), CHUNKS):
        answer(h)
    for h in range(max(CHUNKS, 1), 3):
        output_gate(h - 1)
    wide[...] = jnp.where(diag_out, dot(pick_out, tiled, NN), 0.0).astype(bf16)

    for piece in range(CHUNKS - 1):
        landed(recv2.at[piece], recv_sem2.at[piece])
    for two in range(pairs // 2):
        landed(recv2.at[CHUNKS - 1, :, two], recv_sem2.at[CHUNKS - 1 + two])
        t = jnp.concatenate(
            [
                (recv2[h, :team, two].astype(f32) + recv2[h, team:, two].astype(f32))[:, None]
                for h in range(CHUNKS)
            ],
            axis=1,
        ).reshape(hidden, 16, LANES)
        mean = jnp.sum(t, axis=0, keepdims=True) * (1.0 / hidden)
        d = t - mean
        var = jnp.sum(d * d, axis=0, keepdims=True) * (1.0 / hidden)
        y = d * lax.rsqrt(var + 1e-05)
        for e in range(2):
            qp = 2 * two + e
            flat = y[:, e * EIGHT : (e + 1) * EIGHT, :].reshape(big, LANES)
            lhs = (flat.T * gain_out).astype(bf16)
            res = dot(lhs, wide[...], NN)
            for par in range(2):
                g = gate[(2 * qp + par) * rows : (2 * qp + par + 1) * rows, :]
                val = g * res[par * rows : (par + 1) * rows]
                lo = (par * pairs + qp) * block
                out_ref[:, lo : lo + block] = val.astype(bf16)
    landed(send1.at[:, pl.ds(0, team - 1)], send_sem1.at[0])
    landed(send2.at[:, pl.ds(0, ndev - 1)], send_sem2.at[0])


def write_kernel(update_ref, out_hbm, sem):
    store = pltpu.make_async_copy(update_ref, out_hbm, sem)
    store.start()
    store.wait()


def fused(pair, res_mask, present, ln_in_gain, w_proj, w_gate, ln_out_gain, w_out):
    R, C = lax.axis_size("row"), lax.axis_size("col")
    rows, width = pair.shape
    chans, hidden = w_gate.shape[0], w_out.shape[0]
    cols = width // chans
    groups = cols // EIGHT
    pairs = groups // 2
    ndev = R * C
    team = ndev // 2
    own = hidden // team
    per = own // CHUNKS
    bf16 = jnp.bfloat16
    anywhere = pl.BlockSpec(memory_space=pl.ANY)
    operands = (
        pair, res_mask[None, :], present[None, :], ln_in_gain[None, :], w_proj, w_gate,
        ln_out_gain[None, :], w_out,
    )
    sub = pairs * EIGHT
    update = pl.pallas_call(
        functools.partial(fused_kernel, R, C),
        out_shape=pltpu.VMEM(pair.shape, bf16),
        in_specs=[anywhere] * len(operands),
        out_specs=pl.BlockSpec(memory_space=pltpu.VMEM),
        scratch_shapes=[pltpu.VMEM(value.shape, value.dtype) for value in operands]
        + [
            pltpu.VMEM((groups * rows, EIGHT * chans), bf16),
            pltpu.VMEM((groups * rows, EIGHT * chans), jnp.float32),
            pltpu.VMEM((hidden * EIGHT, EIGHT * chans), bf16),
            pltpu.VMEM((per * EIGHT, groups * rows), jnp.float32),
            pltpu.VMEM((CHUNKS, team, per, 2, sub, LANES), bf16),
            pltpu.VMEM((CHUNKS, team, per, 2, sub, LANES), bf16),
            pltpu.VMEM((CHUNKS, ndev, 2, per, sub // 2, LANES), bf16),
            pltpu.VMEM((CHUNKS, ndev, 2, per, sub // 2, LANES), bf16),
            pltpu.SemaphoreType.DMA((1,)),
            pltpu.SemaphoreType.DMA((CHUNKS,)),
            pltpu.SemaphoreType.DMA((1,)),
            pltpu.SemaphoreType.DMA((CHUNKS + 1,)),
            pltpu.SemaphoreType.DMA((len(operands),)),
        ],
        compiler_params=pltpu.CompilerParams(collective_id=0, has_side_effects=True),
    )(*operands)
    return pl.pallas_call(
        write_kernel,
        out_shape=jax.ShapeDtypeStruct(pair.shape, bf16),
        in_specs=[anywhere],
        out_specs=anywhere,
        scratch_shapes=[pltpu.SemaphoreType.DMA],
        compiler_params=pltpu.CompilerParams(vmem_limit_bytes=WRITE_GRANT),
    )(update)


def fits(R, C, rows, cols, chans, hidden):
    powers = all(n & (n - 1) == 0 for n in (R, C))
    return (
        powers
        and R == C
        and R % 4 == 0
        and rows == cols == LANES // 2
        and chans == hidden == LANES // 2
        and hidden % (R * C // 2 * CHUNKS) == 0
    )


def swapped(value, axis, bit):
    mask = 2**bit
    pairs = [(source, source ^ mask) for source in range(lax.axis_size(axis))]
    return lax.ppermute(value, axis, pairs)


def layer_norm(values, gain):
    mean = jnp.mean(values, axis=-1, keepdims=True)
    var = jnp.mean((values - mean) ** 2, axis=-1, keepdims=True)
    return (values - mean) * lax.rsqrt(var + 1e-05) * gain


def local(pair, res_mask, present, ln_in_gain, w_proj, w_gate, ln_out_gain, w_out):
    rows_here, width = pair.shape
    chans = w_gate.shape[0]
    hidden = w_out.shape[0]
    cols_here = width // chans
    row_count = lax.axis_size("row")
    col_count = lax.axis_size("col")
    if fits(row_count, col_count, rows_here, cols_here, chans, hidden):
        return fused(pair, res_mask, present, ln_in_gain, w_proj, w_gate, ln_out_gain, w_out)
    row_index = lax.axis_index("row")
    col_index = lax.axis_index("col")
    z_tile = pair.astype(jnp.float32).reshape(rows_here, cols_here, chans)
    normed = (
        layer_norm(z_tile, ln_in_gain).astype(jnp.bfloat16).reshape(rows_here * cols_here, chans)
    )
    proj = jnp.dot(normed, w_proj, preferred_element_type=jnp.float32).reshape(
        rows_here, cols_here, 4 * hidden
    )
    weight = (res_mask * present).astype(jnp.float32)
    weight_rows = lax.dynamic_slice_in_dim(weight, row_index * rows_here, rows_here)
    weight_cols = lax.dynamic_slice_in_dim(weight, col_index * cols_here, cols_here)
    pair_mask = (weight_rows[:, None] * weight_cols[None, :])[:, :, None]
    a_tile = (
        pair_mask * jax.nn.sigmoid(proj[:, :, :hidden]) * proj[:, :, hidden : 2 * hidden]
    ).astype(jnp.bfloat16)
    b_tile = (
        pair_mask * jax.nn.sigmoid(proj[:, :, 2 * hidden : 3 * hidden]) * proj[:, :, 3 * hidden :]
    ).astype(jnp.bfloat16)
    gate = jax.nn.sigmoid(jnp.dot(normed, w_gate, preferred_element_type=jnp.float32)).reshape(
        rows_here, cols_here, chans
    )
    factor = 2 if row_count == 4 * col_count else 1
    square_rows = factor * rows_here
    wide_rows = lax.all_gather(a_tile, "col", axis=1, tiled=True)
    spread = wide_rows.reshape(rows_here, row_count // factor, 1, square_rows, hidden)
    spread = jnp.repeat(spread, factor, axis=2).reshape(rows_here, row_count * square_rows, hidden)
    a_square = lax.all_to_all(spread, "row", split_axis=1, concat_axis=0, tiled=True)
    copies = jnp.tile(b_tile, (1, row_count // factor, 1))
    b_square = lax.all_to_all(copies, "row", split_axis=1, concat_axis=0, tiled=True)
    tri_square = jnp.einsum("kic,kjc->ijc", a_square, b_square, preferred_element_type=jnp.float32)
    normed_square = layer_norm(tri_square, ln_out_gain).astype(jnp.bfloat16)
    if factor == 1:
        tri_norm = normed_square
    else:
        parity = row_index % 2
        own_part = lax.dynamic_slice_in_dim(normed_square, parity * rows_here, rows_here, 0)
        other_part = lax.dynamic_slice_in_dim(normed_square, (1 - parity) * rows_here, rows_here, 0)
        received = swapped(other_part, "row", 0)
        tri_norm = jnp.where(
            parity == 0,
            jnp.concatenate([own_part, received], axis=1),
            jnp.concatenate([received, own_part], axis=1),
        )
    flat_norm = tri_norm.reshape(rows_here * cols_here, hidden)
    projected = jnp.dot(flat_norm, w_out, preferred_element_type=jnp.float32).reshape(
        rows_here, cols_here, chans
    )
    return (gate * projected).astype(jnp.bfloat16).reshape(rows_here, cols_here * chans)


def solution(mesh):
    in_specs = (P(("groups", "row"), "col"), P("groups"), P("groups"), P(), P(), P(), P(), P())
    out_specs = P(("groups", "row"), "col")
    return jax.shard_map(local, mesh=mesh, in_specs=in_specs, out_specs=out_specs, check_vma=False)
```

```python
import functools

import jax
import jax.numpy as jnp
from jax import lax
from jax.experimental import pallas as pl
from jax.experimental.pallas import tpu as pltpu
from jax.sharding import PartitionSpec as P

NT = (((1,), (1,)), ((), ()))
NN = (((1,), (0,)), ((), ()))
EIGHT = 8
LANES = 128
SIZES = (1, 1, 2, 2, 2)
WRITE_GRANT = 2**20


def dot(lhs, rhs, dims):
    return lax.dot_general(lhs, rhs, dims, preferred_element_type=jnp.float32)


def flipped(value, mask, count):
    total = 0
    step = 1
    while step < count:
        total = total + ((value // step + mask // step) % 2) * step
        step *= 2
    return total


def lane_pair(left, right, half):
    w = LANES // 2
    return jnp.concatenate(
        [left[:, half * w : (half + 1) * w], right[:, half * w : (half + 1) * w]], axis=1
    )


def iota(shape, dim):
    return lax.broadcasted_iota(jnp.int32, shape, dim)


def fused_kernel(
    R, C, pair_hbm, res_hbm, present_hbm, gain_in_hbm, w_proj_hbm, w_gate_hbm, gain_out_hbm,
    w_out_hbm, out_ref, pair_ref, res_ref, present_ref, gain_in_ref, w_proj_ref, w_gate_ref,
    gain_out_ref, w_out_ref, normed, gate, wide, masks, send1, recv1, send2, recv2,
    send_sem1, recv_sem1, send_sem2, recv_sem2, in_sem,
):
    f32, bf16 = jnp.float32, jnp.bfloat16
    rows = pair_ref.shape[0]
    chans = w_gate_ref.shape[0]
    hidden = w_out_ref.shape[0]
    ndev = R * C
    depth = R // 2
    team = depth * C
    own = hidden // team
    last = len(SIZES) - 1
    start = [sum(SIZES[:h]) for h in range(len(SIZES))]
    groups = normed.shape[0] // rows
    pairs = groups // 2
    block = EIGHT * chans
    half_block = block // 2
    r, c = lax.axis_index("row"), lax.axis_index("col")
    me = r * C + c
    half_row = r // depth * depth
    seat = r % depth * C + c
    half = r // depth

    def mate(n):
        row = half_row + flipped(r % depth, depth - 1 - n // C, depth)
        return row, flipped(c, C - 1 - n % C, C)

    def partner(n):
        return flipped(r, R - 1 - n // C, R), flipped(c, C - 1 - n % C, C)

    def beyond(q, n):
        return (R - 1) * (1 - half) + q * (2 * half - 1), flipped(c, C - 1 - n, C)

    barrier = pltpu.get_barrier_semaphore()

    loads = [
        pltpu.make_async_copy(source, target, in_sem.at[at])
        for at, (source, target) in enumerate(
            (
                (pair_hbm, pair_ref), (gain_in_hbm, gain_in_ref), (gain_out_hbm, gain_out_ref),
                (res_hbm, res_ref), (present_hbm, present_ref), (w_proj_hbm, w_proj_ref),
                (w_gate_hbm, w_gate_ref), (w_out_hbm, w_out_ref),
            )
        )
    ]
    for load in loads:
        load.start()
    def greet(n, carry):
        pr, pc = partner(n)
        pl.semaphore_signal(
            barrier, inc=1, device_id={"row": pr, "col": pc}, device_id_type=pl.DeviceIdType.MESH
        )
        return carry

    lax.fori_loop(0, ndev - 1, greet, 0)
    same = (iota((half_block, half_block), 0) // chans) == (
        iota((half_block, half_block), 1) // chans
    )
    ones = same.astype(f32).astype(bf16)
    for load in loads[1:]:
        load.wait()
    eye = iota((chans, chans), 0) == iota((chans, chans), 1)
    sub_id, lane_in = iota((chans, block), 0), iota((chans, block), 1)

    def over_lanes(gain_ref, match):
        column = jnp.sum(jnp.where(eye, gain_ref[...], 0.0), axis=1, keepdims=True)
        return jnp.sum(jnp.where(match, column, 0.0), axis=0, keepdims=True)

    gain_in = over_lanes(gain_in_ref, lane_in % chans == sub_id)
    gain_out = over_lanes(gain_out_ref, lane_in // EIGHT == sub_id)

    count = res_ref.shape[1]
    alive = (res_ref[...] * present_ref[...]).astype(f32)
    wide_lanes = groups * rows
    res_id, lane = iota((count, wide_lanes), 0), iota((count, wide_lanes), 1)
    group = (lane // rows) % 2 * pairs + lane // LANES
    is_row = (res_id == r * rows + lane % rows).astype(f32).astype(bf16)
    is_col = (res_id // EIGHT == c * groups + group).astype(f32).astype(bf16)
    shape = (max(SIZES) * EIGHT, count)
    phase = iota(shape, 0) % EIGHT == iota(shape, 1) % EIGHT
    rows_alive = dot(jnp.broadcast_to(alive, shape).astype(bf16), is_row, NN)
    masks[...] = rows_alive * dot(jnp.where(phase, alive, 0.0).astype(bf16), is_col, NN)

    stacked = jnp.concatenate([w_proj_ref[...]] * EIGHT, axis=0)
    out_chans = w_proj_ref.shape[1]

    def weights_of(h):
        part = SIZES[h] * EIGHT
        n_rows = team * 4 * part
        diag = (iota((n_rows, block), 0) % EIGHT) == (iota((n_rows, block), 1) // chans)
        row_id = iota((n_rows, out_chans), 0)
        target = row_id // part % 4 * hidden + row_id // (4 * part) * own + row_id % part // EIGHT
        target = iota((n_rows, out_chans), 1) - target
        pick = (target == start[h]).astype(f32).astype(bf16)
        return jnp.where(diag, dot(pick, stacked, NT), 0.0).astype(bf16)

    first_weights = weights_of(0)

    loads[0].wait()
    for h in range(2):
        parts = []
        for qp in range(pairs):
            for par in range(2):
                lo = (par * pairs + qp) * block + h * half_block
                parts.append(pair_ref[:, lo : lo + half_block])
        x = jnp.concatenate(parts, axis=0)
        d = x.astype(f32) - dot(x, ones, NN) * (1.0 / chans)
        sq = d * d
        hi = sq.astype(bf16)
        lo_part = (sq - hi.astype(f32)).astype(bf16)
        var = (dot(hi, ones, NN) + dot(lo_part, ones, NN)) * (1.0 / chans)
        y = d * lax.rsqrt(var + 1e-05) * gain_in[:, h * half_block : (h + 1) * half_block]
        normed[:, h * half_block : (h + 1) * half_block] = y.astype(bf16)

    def project(h):
        per = SIZES[h]
        part = per * EIGHT
        res = dot(weights_of(h) if h > 0 else first_weights, normed[...], NT)
        mask = masks[:part]
        for dest in range(team):
            for which in range(2):
                lo = (4 * dest + 2 * which) * part
                g, v = res[lo : lo + part], res[lo + part : lo + 2 * part]
                val = mask * jax.nn.sigmoid(g) * v
                for ch in range(per):
                    tile = jnp.concatenate(
                        [
                            val[ch * EIGHT : (ch + 1) * EIGHT, qp * LANES : (qp + 1) * LANES]
                            for qp in range(pairs)
                        ],
                        axis=0,
                    )
                    send1[dest, start[h] + ch, which] = tile.astype(bf16)

    def remote(source, target, ssem, rsem, where):
        return pltpu.make_async_remote_copy(
            src_ref=source, dst_ref=target, send_sem=ssem, recv_sem=rsem,
            device_id={"row": where[0], "col": where[1]}, device_id_type=pl.DeviceIdType.MESH,
        )

    def span(h):
        return pl.ds(start[h], SIZES[h])

    def copy1(h, n):
        where = mate(n)
        p = (where[0] - half_row) * C + where[1]
        return remote(
            send1.at[p, span(h)], recv1.at[seat, span(h)], send_sem1, recv_sem1.at[h], where
        )

    def views(piece, p):
        if piece < last:
            return send2.at[p, span(piece)], recv2.at[me, span(piece)]
        two = piece - last
        return send2.at[p, span(last), two], recv2.at[me, span(last), two]

    def copy2(piece, where):
        source, target = views(piece, where[0] * C + where[1])
        return remote(source, target, send_sem2, recv_sem2.at[piece], where)

    def each(total, body):
        def run(n, carry):
            body(n)
            return carry

        lax.fori_loop(0, total, run, 0)

    gate_rows = jnp.concatenate([w_gate_ref[...]] * (half_block // chans), axis=0)
    spread = ((iota((chans, block), 1) % chans) == iota((chans, block), 0)).astype(f32).astype(bf16)
    w_gate4 = jnp.where(same, dot(gate_rows, spread[:, :half_block], NN), 0.0).astype(bf16)

    def output_gate(h):
        cols = slice(h * half_block, (h + 1) * half_block)
        gate[:, cols] = jax.nn.sigmoid(dot(normed[:, cols], w_gate4, NN))

    def landed(ref, sem):
        pltpu.make_async_copy(ref, ref, sem).wait()

    tiled = dot(w_out_ref[...], spread, NN).astype(bf16)
    big = hidden * EIGHT
    pick_out = ((iota((big, hidden), 0) // EIGHT) == iota((big, hidden), 1)).astype(f32).astype(bf16)
    diag_out = (iota((big, block), 0) % EIGHT) == (iota((big, block), 1) // chans)

    sub = pairs * EIGHT

    def multiply(ch):
        full = []
        for which in range(2):
            by_parity = [[], []]
            for rp in range(depth // 2):
                one, two = (
                    jnp.concatenate(
                        [recv1[(2 * rp + e) * C + cc, ch, which] for cc in range(C)], axis=0
                    ).astype(f32)
                    for e in range(2)
                )
                for par in range(2):
                    by_parity[par].append(lane_pair(one, two, par).astype(bf16))
            full.append([jnp.concatenate(p, axis=1) for p in by_parity])
        a_rows = jnp.concatenate(
            [full[0][par][cc * sub : (cc + 1) * sub] for cc in range(C) for par in range(2)], axis=0
        )
        even, odd = (dot(full[1][par], a_rows, NT) for par in range(2))
        for rp in range(R // 2):
            cols = slice(rp * LANES, (rp + 1) * LANES)
            for e in range(2):
                tile = lane_pair(even[:, cols], odd[:, cols], e).astype(bf16)
                for cc in range(C):
                    for two in range(2):
                        lo = cc * sub + two * (sub // 2)
                        send2[(2 * rp + e) * C + cc, ch, two] = tile[lo : lo + sub // 2]

    def begin(h):
        each(team - 1, lambda n: copy1(h, n).start())
        pltpu.make_async_copy(
            send1.at[seat, span(h)], recv1.at[seat, span(h)], recv_sem1.at[h]
        ).start()

    def answer(h):
        landed(recv1.at[:, span(h)], recv_sem1.at[h])
        for ch in range(SIZES[h]):
            multiply(start[h] + ch)
        pieces = (h,) if h < last else (h, h + 1)
        for q in range(depth):
            for piece in pieces:
                each(C, lambda n, q=q, piece=piece: copy2(piece, beyond(q, n)).start())
        for piece in pieces:
            each(team - 1, lambda n, piece=piece: copy2(piece, partner(n + team)).start())
            source, target = views(piece, me)
            pltpu.make_async_copy(source, target, recv_sem2.at[piece]).start()

    for h in range(len(SIZES)):
        project(h)
        if h == 0:
            pl.semaphore_wait(barrier, ndev - 1)
        if h in (1, 2):
            output_gate(h - 1)
        begin(h)
        if h >= 2:
            answer(h - 2)
    for h in range(len(SIZES) - 2, len(SIZES)):
        answer(h)
    wide[...] = jnp.where(diag_out, dot(pick_out, tiled, NN), 0.0).astype(bf16)

    for piece in range(last):
        landed(recv2.at[:, span(piece)], recv_sem2.at[piece])
    for two in range(pairs // 2):
        landed(recv2.at[:, span(last), two], recv_sem2.at[last + two])
        t = recv2[:team, :, two].astype(f32) + recv2[team:, :, two].astype(f32)
        t = t.reshape(hidden, 16, LANES)
        mean = jnp.sum(t, axis=0, keepdims=True) * (1.0 / hidden)
        d = t - mean
        var = jnp.sum(d * d, axis=0, keepdims=True) * (1.0 / hidden)
        y = d * lax.rsqrt(var + 1e-05)
        for e in range(2):
            qp = 2 * two + e
            flat = y[:, e * EIGHT : (e + 1) * EIGHT, :].reshape(big, LANES)
            lhs = (flat.T * gain_out).astype(bf16)
            res = dot(lhs, wide[...], NN)
            for par in range(2):
                g = gate[(2 * qp + par) * rows : (2 * qp + par + 1) * rows, :]
                val = g * res[par * rows : (par + 1) * rows]
                lo = (par * pairs + qp) * block
                out_ref[:, lo : lo + block] = val.astype(bf16)
    landed(send1.at[pl.ds(0, team - 1)], send_sem1)
    landed(send2.at[pl.ds(0, ndev - 1)], send_sem2)


def write_kernel(update_ref, out_hbm, sem):
    store = pltpu.make_async_copy(update_ref, out_hbm, sem)
    store.start()
    store.wait()


def fused(pair, res_mask, present, ln_in_gain, w_proj, w_gate, ln_out_gain, w_out):
    R, C = lax.axis_size("row"), lax.axis_size("col")
    rows, width = pair.shape
    chans, hidden = w_gate.shape[0], w_out.shape[0]
    cols = width // chans
    groups = cols // EIGHT
    pairs = groups // 2
    ndev = R * C
    team = ndev // 2
    own = sum(SIZES)
    bf16 = jnp.bfloat16
    anywhere = pl.BlockSpec(memory_space=pl.ANY)
    operands = (
        pair, res_mask[None, :], present[None, :], ln_in_gain[None, :], w_proj, w_gate,
        ln_out_gain[None, :], w_out,
    )
    sub = pairs * EIGHT
    update = pl.pallas_call(
        functools.partial(fused_kernel, R, C),
        out_shape=pltpu.VMEM(pair.shape, bf16),
        in_specs=[anywhere] * len(operands),
        out_specs=pl.BlockSpec(memory_space=pltpu.VMEM),
        scratch_shapes=[pltpu.VMEM(value.shape, value.dtype) for value in operands]
        + [
            pltpu.VMEM((groups * rows, EIGHT * chans), bf16),
            pltpu.VMEM((groups * rows, EIGHT * chans), jnp.float32),
            pltpu.VMEM((hidden * EIGHT, EIGHT * chans), bf16),
            pltpu.VMEM((max(SIZES) * EIGHT, groups * rows), jnp.float32),
            pltpu.VMEM((team, own, 2, sub, LANES), bf16),
            pltpu.VMEM((team, own, 2, sub, LANES), bf16),
            pltpu.VMEM((ndev, own, 2, sub // 2, LANES), bf16),
            pltpu.VMEM((ndev, own, 2, sub // 2, LANES), bf16),
            pltpu.SemaphoreType.DMA,
            pltpu.SemaphoreType.DMA((len(SIZES),)),
            pltpu.SemaphoreType.DMA,
            pltpu.SemaphoreType.DMA((len(SIZES) + 1,)),
            pltpu.SemaphoreType.DMA((len(operands),)),
        ],
        compiler_params=pltpu.CompilerParams(collective_id=0, has_side_effects=True),
    )(*operands)
    return pl.pallas_call(
        write_kernel,
        out_shape=jax.ShapeDtypeStruct(pair.shape, bf16),
        in_specs=[anywhere],
        out_specs=anywhere,
        scratch_shapes=[pltpu.SemaphoreType.DMA],
        compiler_params=pltpu.CompilerParams(vmem_limit_bytes=WRITE_GRANT),
    )(update)


def fits(R, C, rows, cols, chans, hidden):
    powers = all(n & (n - 1) == 0 for n in (R, C))
    return (
        powers
        and R == C
        and R % 4 == 0
        and rows == cols == LANES // 2
        and chans == hidden == LANES // 2
        and R // 2 == 2
        and hidden == R * C // 2 * sum(SIZES)
    )


def swapped(value, axis, bit):
    mask = 2**bit
    pairs = [(source, source ^ mask) for source in range(lax.axis_size(axis))]
    return lax.ppermute(value, axis, pairs)


def layer_norm(values, gain):
    mean = jnp.mean(values, axis=-1, keepdims=True)
    var = jnp.mean((values - mean) ** 2, axis=-1, keepdims=True)
    return (values - mean) * lax.rsqrt(var + 1e-05) * gain


def local(pair, res_mask, present, ln_in_gain, w_proj, w_gate, ln_out_gain, w_out):
    rows_here, width = pair.shape
    chans = w_gate.shape[0]
    hidden = w_out.shape[0]
    cols_here = width // chans
    row_count = lax.axis_size("row")
    col_count = lax.axis_size("col")
    if fits(row_count, col_count, rows_here, cols_here, chans, hidden):
        return fused(pair, res_mask, present, ln_in_gain, w_proj, w_gate, ln_out_gain, w_out)
    row_index = lax.axis_index("row")
    col_index = lax.axis_index("col")
    z_tile = pair.astype(jnp.float32).reshape(rows_here, cols_here, chans)
    normed = (
        layer_norm(z_tile, ln_in_gain).astype(jnp.bfloat16).reshape(rows_here * cols_here, chans)
    )
    proj = jnp.dot(normed, w_proj, preferred_element_type=jnp.float32).reshape(
        rows_here, cols_here, 4 * hidden
    )
    weight = (res_mask * present).astype(jnp.float32)
    weight_rows = lax.dynamic_slice_in_dim(weight, row_index * rows_here, rows_here)
    weight_cols = lax.dynamic_slice_in_dim(weight, col_index * cols_here, cols_here)
    pair_mask = (weight_rows[:, None] * weight_cols[None, :])[:, :, None]
    a_tile = (
        pair_mask * jax.nn.sigmoid(proj[:, :, :hidden]) * proj[:, :, hidden : 2 * hidden]
    ).astype(jnp.bfloat16)
    b_tile = (
        pair_mask * jax.nn.sigmoid(proj[:, :, 2 * hidden : 3 * hidden]) * proj[:, :, 3 * hidden :]
    ).astype(jnp.bfloat16)
    gate = jax.nn.sigmoid(jnp.dot(normed, w_gate, preferred_element_type=jnp.float32)).reshape(
        rows_here, cols_here, chans
    )
    factor = 2 if row_count == 4 * col_count else 1
    square_rows = factor * rows_here
    wide_rows = lax.all_gather(a_tile, "col", axis=1, tiled=True)
    spread = wide_rows.reshape(rows_here, row_count // factor, 1, square_rows, hidden)
    spread = jnp.repeat(spread, factor, axis=2).reshape(rows_here, row_count * square_rows, hidden)
    a_square = lax.all_to_all(spread, "row", split_axis=1, concat_axis=0, tiled=True)
    copies = jnp.tile(b_tile, (1, row_count // factor, 1))
    b_square = lax.all_to_all(copies, "row", split_axis=1, concat_axis=0, tiled=True)
    tri_square = jnp.einsum("kic,kjc->ijc", a_square, b_square, preferred_element_type=jnp.float32)
    normed_square = layer_norm(tri_square, ln_out_gain).astype(jnp.bfloat16)
    if factor == 1:
        tri_norm = normed_square
    else:
        parity = row_index % 2
        own_part = lax.dynamic_slice_in_dim(normed_square, parity * rows_here, rows_here, 0)
        other_part = lax.dynamic_slice_in_dim(normed_square, (1 - parity) * rows_here, rows_here, 0)
        received = swapped(other_part, "row", 0)
        tri_norm = jnp.where(
            parity == 0,
            jnp.concatenate([own_part, received], axis=1),
            jnp.concatenate([received, own_part], axis=1),
        )
    flat_norm = tri_norm.reshape(rows_here * cols_here, hidden)
    projected = jnp.dot(flat_norm, w_out, preferred_element_type=jnp.float32).reshape(
        rows_here, cols_here, chans
    )
    return (gate * projected).astype(jnp.bfloat16).reshape(rows_here, cols_here * chans)


def solution(mesh):
    in_specs = (P(("groups", "row"), "col"), P("groups"), P("groups"), P(), P(), P(), P(), P())
    out_specs = P(("groups", "row"), "col")
    return jax.shard_map(local, mesh=mesh, in_specs=in_specs, out_specs=out_specs, check_vma=False)
```

```python
import functools

import jax
import jax.numpy as jnp
from jax import lax
from jax.experimental import pallas as pl
from jax.experimental.pallas import tpu as pltpu
from jax.sharding import PartitionSpec as P

NT = (((1,), (1,)), ((), ()))
NN = (((1,), (0,)), ((), ()))
EIGHT = 8
LANES = 128
SIZES = (1, 1, 2, 2, 2)
WRITE_GRANT = 2**20


def dot(lhs, rhs, dims):
    return lax.dot_general(lhs, rhs, dims, preferred_element_type=jnp.float32)


def flipped(value, mask, count):
    total = 0
    step = 1
    while step < count:
        total = total + ((value // step + mask // step) % 2) * step
        step *= 2
    return total


def lane_pair(left, right, half):
    w = LANES // 2
    return jnp.concatenate(
        [left[:, half * w : (half + 1) * w], right[:, half * w : (half + 1) * w]], axis=1
    )


def iota(shape, dim):
    return lax.broadcasted_iota(jnp.int32, shape, dim)


def fused_kernel(
    R, C, pair_hbm, res_hbm, present_hbm, gain_in_hbm, w_proj_hbm, w_gate_hbm, gain_out_hbm,
    w_out_hbm, out_ref, pair_ref, res_ref, present_ref, gain_in_ref, w_proj_ref, w_gate_ref,
    gain_out_ref, w_out_ref, normed, gate, wide, masks, send1, recv1, send2, recv2, joined,
    send_sem1, recv_sem1, send_sem2, recv_sem2, join_sem, in_sem,
):
    f32, bf16 = jnp.float32, jnp.bfloat16
    rows = pair_ref.shape[0]
    chans = w_gate_ref.shape[0]
    hidden = w_out_ref.shape[0]
    ndev = R * C
    depth = R // 2
    team = depth * C
    own = hidden // team
    last = len(SIZES) - 1
    folds = last
    start = [sum(SIZES[:h]) for h in range(len(SIZES))]
    groups = normed.shape[0] // rows
    pairs = groups // 2
    block = EIGHT * chans
    half_block = block // 2
    r, c = lax.axis_index("row"), lax.axis_index("col")
    me = r * C + c
    half_row = r // depth * depth
    seat = r % depth * C + c
    half = r // depth
    middle = (r % depth + half) % 2

    def mate(n):
        row = half_row + flipped(r % depth, depth - 1 - n // C, depth)
        return row, flipped(c, C - 1 - n % C, C)

    def partner(n):
        return flipped(r, R - 1 - n // C, R), flipped(c, C - 1 - n % C, C)

    def beyond(q, n):
        return (R - 1) * (1 - half) + q * (2 * half - 1), flipped(c, C - 1 - n, C)

    barrier = pltpu.get_barrier_semaphore()

    loads = [
        pltpu.make_async_copy(source, target, in_sem.at[at])
        for at, (source, target) in enumerate(
            (
                (pair_hbm, pair_ref), (gain_in_hbm, gain_in_ref), (gain_out_hbm, gain_out_ref),
                (res_hbm, res_ref), (present_hbm, present_ref), (w_proj_hbm, w_proj_ref),
                (w_gate_hbm, w_gate_ref), (w_out_hbm, w_out_ref),
            )
        )
    ]
    for load in loads:
        load.start()
    def greet(n, carry):
        pr, pc = partner(n)
        pl.semaphore_signal(
            barrier, inc=1, device_id={"row": pr, "col": pc}, device_id_type=pl.DeviceIdType.MESH
        )
        return carry

    lax.fori_loop(0, ndev - 1, greet, 0)
    same = (iota((half_block, half_block), 0) // chans) == (
        iota((half_block, half_block), 1) // chans
    )
    ones = same.astype(f32).astype(bf16)
    for load in loads[1:]:
        load.wait()
    eye = iota((chans, chans), 0) == iota((chans, chans), 1)
    sub_id, lane_in = iota((chans, block), 0), iota((chans, block), 1)

    def over_lanes(gain_ref, match):
        column = jnp.sum(jnp.where(eye, gain_ref[...], 0.0), axis=1, keepdims=True)
        return jnp.sum(jnp.where(match, column, 0.0), axis=0, keepdims=True)

    gain_in = over_lanes(gain_in_ref, lane_in % chans == sub_id)
    gain_out = over_lanes(gain_out_ref, lane_in // EIGHT == sub_id)

    count = res_ref.shape[1]
    alive = (res_ref[...] * present_ref[...]).astype(f32)
    wide_lanes = groups * rows
    res_id, lane = iota((count, wide_lanes), 0), iota((count, wide_lanes), 1)
    group = (lane // rows) % 2 * pairs + lane // LANES
    is_row = (res_id == r * rows + lane % rows).astype(f32).astype(bf16)
    is_col = (res_id // EIGHT == c * groups + group).astype(f32).astype(bf16)
    shape = (max(SIZES) * EIGHT, count)
    phase = iota(shape, 0) % EIGHT == iota(shape, 1) % EIGHT
    rows_alive = dot(jnp.broadcast_to(alive, shape).astype(bf16), is_row, NN)
    masks[...] = rows_alive * dot(jnp.where(phase, alive, 0.0).astype(bf16), is_col, NN)

    stacked = jnp.concatenate([w_proj_ref[...]] * EIGHT, axis=0)
    out_chans = w_proj_ref.shape[1]

    def weights_of(h):
        part = SIZES[h] * EIGHT
        n_rows = team * 4 * part
        diag = (iota((n_rows, block), 0) % EIGHT) == (iota((n_rows, block), 1) // chans)
        row_id = iota((n_rows, out_chans), 0)
        target = row_id // part % 4 * hidden + row_id // (4 * part) * own + row_id % part // EIGHT
        target = iota((n_rows, out_chans), 1) - target
        pick = (target == start[h]).astype(f32).astype(bf16)
        return jnp.where(diag, dot(pick, stacked, NT), 0.0).astype(bf16)

    first_weights = weights_of(0)

    @pl.when(middle == 0)
    def _():
        for cc in range(C):
            recv2[(R - 1 - r) * C + cc, : start[folds]] = jnp.zeros(
                (start[folds],) + recv2.shape[2:], bf16
            )

    loads[0].wait()
    for h in range(2):
        parts = []
        for qp in range(pairs):
            for par in range(2):
                lo = (par * pairs + qp) * block + h * half_block
                parts.append(pair_ref[:, lo : lo + half_block])
        x = jnp.concatenate(parts, axis=0)
        d = x.astype(f32) - dot(x, ones, NN) * (1.0 / chans)
        sq = d * d
        hi = sq.astype(bf16)
        lo_part = (sq - hi.astype(f32)).astype(bf16)
        var = (dot(hi, ones, NN) + dot(lo_part, ones, NN)) * (1.0 / chans)
        y = d * lax.rsqrt(var + 1e-05) * gain_in[:, h * half_block : (h + 1) * half_block]
        normed[:, h * half_block : (h + 1) * half_block] = y.astype(bf16)

    def project(h):
        per = SIZES[h]
        part = per * EIGHT
        res = dot(weights_of(h) if h > 0 else first_weights, normed[...], NT)
        mask = masks[:part]
        for dest in range(team):
            for which in range(2):
                lo = (4 * dest + 2 * which) * part
                g, v = res[lo : lo + part], res[lo + part : lo + 2 * part]
                val = mask * jax.nn.sigmoid(g) * v
                for ch in range(per):
                    tile = jnp.concatenate(
                        [
                            val[ch * EIGHT : (ch + 1) * EIGHT, qp * LANES : (qp + 1) * LANES]
                            for qp in range(pairs)
                        ],
                        axis=0,
                    )
                    send1[dest, start[h] + ch, which] = tile.astype(bf16)

    def remote(source, target, ssem, rsem, where):
        return pltpu.make_async_remote_copy(
            src_ref=source, dst_ref=target, send_sem=ssem, recv_sem=rsem,
            device_id={"row": where[0], "col": where[1]}, device_id_type=pl.DeviceIdType.MESH,
        )

    def span(h):
        return pl.ds(start[h], SIZES[h])

    def copy1(h, n):
        where = mate(n)
        p = (where[0] - half_row) * C + where[1]
        return remote(
            send1.at[p, span(h)], recv1.at[seat, span(h)], send_sem1, recv_sem1.at[h], where
        )

    def views(piece, p):
        if piece < last:
            return send2.at[p, span(piece)], recv2.at[me, span(piece)]
        two = piece - last
        return send2.at[p, span(last), two], recv2.at[me, span(last), two]

    def copy2(piece, where):
        source, target = views(piece, where[0] * C + where[1])
        return remote(source, target, send_sem2, recv_sem2.at[piece], where)

    def each(total, body):
        def run(n, carry):
            body(n)
            return carry

        lax.fori_loop(0, total, run, 0)

    gate_rows = jnp.concatenate([w_gate_ref[...]] * (half_block // chans), axis=0)
    spread = ((iota((chans, block), 1) % chans) == iota((chans, block), 0)).astype(f32).astype(bf16)
    w_gate4 = jnp.where(same, dot(gate_rows, spread[:, :half_block], NN), 0.0).astype(bf16)

    def output_gate(h):
        cols = slice(h * half_block, (h + 1) * half_block)
        gate[:, cols] = jax.nn.sigmoid(dot(normed[:, cols], w_gate4, NN))

    def landed(ref, sem):
        pltpu.make_async_copy(ref, ref, sem).wait()

    tiled = dot(w_out_ref[...], spread, NN).astype(bf16)
    big = hidden * EIGHT
    pick_out = ((iota((big, hidden), 0) // EIGHT) == iota((big, hidden), 1)).astype(f32).astype(bf16)
    diag_out = (iota((big, block), 0) % EIGHT) == (iota((big, block), 1) // chans)

    sub = pairs * EIGHT

    def multiply(ch):
        full = []
        for which in range(2):
            by_parity = [[], []]
            for rp in range(depth // 2):
                one, two = (
                    jnp.concatenate(
                        [recv1[(2 * rp + e) * C + cc, ch, which] for cc in range(C)], axis=0
                    ).astype(f32)
                    for e in range(2)
                )
                for par in range(2):
                    by_parity[par].append(lane_pair(one, two, par).astype(bf16))
            full.append([jnp.concatenate(p, axis=1) for p in by_parity])
        a_rows = jnp.concatenate(
            [full[0][par][cc * sub : (cc + 1) * sub] for cc in range(C) for par in range(2)], axis=0
        )
        even, odd = (dot(full[1][par], a_rows, NT) for par in range(2))
        for rp in range(R // 2):
            cols = slice(rp * LANES, (rp + 1) * LANES)
            for e in range(2):
                tile = lane_pair(even[:, cols], odd[:, cols], e).astype(bf16)
                for cc in range(C):
                    for two in range(2):
                        lo = cc * sub + two * (sub // 2)
                        send2[(2 * rp + e) * C + cc, ch, two] = tile[lo : lo + sub // 2]

    def piece_of(ref, row, piece):
        if piece < last:
            return ref.at[row, span(piece)]
        return ref.at[row, span(last), piece - last]

    def copy_join(piece, n):
        row, col = beyond(0, n)
        return remote(
            piece_of(send2, row * C + col, piece), piece_of(joined, col, piece),
            send_sem2, join_sem.at[piece], (beyond(1, n)[0], c),
        )

    def join(piece):
        chans_of = slice(start[min(piece, last)], start[min(piece, last)] + SIZES[min(piece, last)])
        two = slice(0, 2) if piece < last else slice(piece - last, piece - last + 1)
        every = joined.at[:, span(piece)] if piece < last else joined.at[:, span(last), piece - last]
        landed(every, join_sem.at[piece])
        row = flipped(r, 1, R)
        for cc in range(C):
            both = send2[row * C + cc, chans_of, two].astype(f32)
            both = both + joined[cc, chans_of, two].astype(f32)
            send2[row * C + cc, chans_of, two] = both.astype(bf16)
        each(C, lambda n: copy2(piece, partner(n + team)).start())

    def begin(h):
        each(team - 1, lambda n: copy1(h, n).start())
        pltpu.make_async_copy(
            send1.at[seat, span(h)], recv1.at[seat, span(h)], recv_sem1.at[h]
        ).start()

    def answer(h):
        landed(recv1.at[:, span(h)], recv_sem1.at[h])
        for ch in range(SIZES[h]):
            multiply(start[h] + ch)
        pieces = (h,) if h < last else (h, h + 1)
        if h < folds:

            @pl.when(middle == 1)
            def _():
                each(C, lambda n: copy2(h, beyond(0, n)).start())

            @pl.when(middle == 0)
            def _():
                each(C, lambda n: copy_join(h, n).start())

            each(C, lambda n: copy2(h, beyond(1, n)).start())

            @pl.when(middle == 0)
            def _():
                each(C, lambda n: copy2(h, partner(n + team)).start())

        else:
            for q in range(depth):
                for piece in pieces:
                    each(C, lambda n, q=q, piece=piece: copy2(piece, beyond(q, n)).start())
            for piece in pieces:
                each(C, lambda n, piece=piece: copy2(piece, partner(n + team)).start())
        for piece in pieces:
            each(C - 1, lambda n, piece=piece: copy2(piece, partner(n + team + C)).start())
            source, target = views(piece, me)
            pltpu.make_async_copy(source, target, recv_sem2.at[piece]).start()

    for h in range(len(SIZES)):
        project(h)
        if h == 0:
            pl.semaphore_wait(barrier, ndev - 1)
        if h in (1, 2):
            output_gate(h - 1)
        begin(h)
        if h >= 2:
            answer(h - 2)
    for h in range(len(SIZES) - 2, len(SIZES)):
        answer(h)
    wide[...] = jnp.where(diag_out, dot(pick_out, tiled, NN), 0.0).astype(bf16)

    @pl.when(middle == 1)
    def _():
        for piece in range(folds):
            join(piece)

    def arrived(piece):
        if piece >= folds:
            landed(piece_of(recv2, slice(None), piece), recv_sem2.at[piece])
            return
        for kind, slots in ((0, pl.ds(0, ndev - C)), (1, pl.ds(0, ndev))):

            @pl.when(middle == kind)
            def _():
                landed(piece_of(recv2, slots, piece), recv_sem2.at[piece])

    for piece in range(last):
        arrived(piece)
    for two in range(pairs // 2):
        arrived(last + two)
        t = recv2[:team, :, two].astype(f32) + recv2[team:, :, two].astype(f32)
        t = t.reshape(hidden, 16, LANES)
        mean = jnp.sum(t, axis=0, keepdims=True) * (1.0 / hidden)
        d = t - mean
        var = jnp.sum(d * d, axis=0, keepdims=True) * (1.0 / hidden)
        y = d * lax.rsqrt(var + 1e-05)
        for e in range(2):
            qp = 2 * two + e
            flat = y[:, e * EIGHT : (e + 1) * EIGHT, :].reshape(big, LANES)
            lhs = (flat.T * gain_out).astype(bf16)
            res = dot(lhs, wide[...], NN)
            for par in range(2):
                g = gate[(2 * qp + par) * rows : (2 * qp + par + 1) * rows, :]
                val = g * res[par * rows : (par + 1) * rows]
                lo = (par * pairs + qp) * block
                out_ref[:, lo : lo + block] = val.astype(bf16)
    landed(send1.at[pl.ds(0, team - 1)], send_sem1)
    landed(send2.at[pl.ds(0, ndev - 1)], send_sem2)


def write_kernel(update_ref, out_hbm, sem):
    store = pltpu.make_async_copy(update_ref, out_hbm, sem)
    store.start()
    store.wait()


def fused(pair, res_mask, present, ln_in_gain, w_proj, w_gate, ln_out_gain, w_out):
    R, C = lax.axis_size("row"), lax.axis_size("col")
    rows, width = pair.shape
    chans, hidden = w_gate.shape[0], w_out.shape[0]
    cols = width // chans
    groups = cols // EIGHT
    pairs = groups // 2
    ndev = R * C
    team = ndev // 2
    own = sum(SIZES)
    bf16 = jnp.bfloat16
    anywhere = pl.BlockSpec(memory_space=pl.ANY)
    operands = (
        pair, res_mask[None, :], present[None, :], ln_in_gain[None, :], w_proj, w_gate,
        ln_out_gain[None, :], w_out,
    )
    sub = pairs * EIGHT
    update = pl.pallas_call(
        functools.partial(fused_kernel, R, C),
        out_shape=pltpu.VMEM(pair.shape, bf16),
        in_specs=[anywhere] * len(operands),
        out_specs=pl.BlockSpec(memory_space=pltpu.VMEM),
        scratch_shapes=[pltpu.VMEM(value.shape, value.dtype) for value in operands]
        + [
            pltpu.VMEM((groups * rows, EIGHT * chans), bf16),
            pltpu.VMEM((groups * rows, EIGHT * chans), jnp.float32),
            pltpu.VMEM((hidden * EIGHT, EIGHT * chans), bf16),
            pltpu.VMEM((max(SIZES) * EIGHT, groups * rows), jnp.float32),
            pltpu.VMEM((team, own, 2, sub, LANES), bf16),
            pltpu.VMEM((team, own, 2, sub, LANES), bf16),
            pltpu.VMEM((ndev, own, 2, sub // 2, LANES), bf16),
            pltpu.VMEM((ndev, own, 2, sub // 2, LANES), bf16),
            pltpu.VMEM((C, own, 2, sub // 2, LANES), bf16),
            pltpu.SemaphoreType.DMA,
            pltpu.SemaphoreType.DMA((len(SIZES),)),
            pltpu.SemaphoreType.DMA,
            pltpu.SemaphoreType.DMA((len(SIZES) + 1,)),
            pltpu.SemaphoreType.DMA((len(SIZES),)),
            pltpu.SemaphoreType.DMA((len(operands),)),
        ],
        compiler_params=pltpu.CompilerParams(collective_id=0, has_side_effects=True),
    )(*operands)
    return pl.pallas_call(
        write_kernel,
        out_shape=jax.ShapeDtypeStruct(pair.shape, bf16),
        in_specs=[anywhere],
        out_specs=anywhere,
        scratch_shapes=[pltpu.SemaphoreType.DMA],
        compiler_params=pltpu.CompilerParams(vmem_limit_bytes=WRITE_GRANT),
    )(update)


def fits(R, C, rows, cols, chans, hidden):
    powers = all(n & (n - 1) == 0 for n in (R, C))
    return (
        powers
        and R == C
        and R % 4 == 0
        and rows == cols == LANES // 2
        and chans == hidden == LANES // 2
        and R // 2 == 2
        and hidden == R * C // 2 * sum(SIZES)
    )


def swapped(value, axis, bit):
    mask = 2**bit
    pairs = [(source, source ^ mask) for source in range(lax.axis_size(axis))]
    return lax.ppermute(value, axis, pairs)


def layer_norm(values, gain):
    mean = jnp.mean(values, axis=-1, keepdims=True)
    var = jnp.mean((values - mean) ** 2, axis=-1, keepdims=True)
    return (values - mean) * lax.rsqrt(var + 1e-05) * gain


def local(pair, res_mask, present, ln_in_gain, w_proj, w_gate, ln_out_gain, w_out):
    rows_here, width = pair.shape
    chans = w_gate.shape[0]
    hidden = w_out.shape[0]
    cols_here = width // chans
    row_count = lax.axis_size("row")
    col_count = lax.axis_size("col")
    if fits(row_count, col_count, rows_here, cols_here, chans, hidden):
        return fused(pair, res_mask, present, ln_in_gain, w_proj, w_gate, ln_out_gain, w_out)
    row_index = lax.axis_index("row")
    col_index = lax.axis_index("col")
    z_tile = pair.astype(jnp.float32).reshape(rows_here, cols_here, chans)
    normed = (
        layer_norm(z_tile, ln_in_gain).astype(jnp.bfloat16).reshape(rows_here * cols_here, chans)
    )
    proj = jnp.dot(normed, w_proj, preferred_element_type=jnp.float32).reshape(
        rows_here, cols_here, 4 * hidden
    )
    weight = (res_mask * present).astype(jnp.float32)
    weight_rows = lax.dynamic_slice_in_dim(weight, row_index * rows_here, rows_here)
    weight_cols = lax.dynamic_slice_in_dim(weight, col_index * cols_here, cols_here)
    pair_mask = (weight_rows[:, None] * weight_cols[None, :])[:, :, None]
    a_tile = (
        pair_mask * jax.nn.sigmoid(proj[:, :, :hidden]) * proj[:, :, hidden : 2 * hidden]
    ).astype(jnp.bfloat16)
    b_tile = (
        pair_mask * jax.nn.sigmoid(proj[:, :, 2 * hidden : 3 * hidden]) * proj[:, :, 3 * hidden :]
    ).astype(jnp.bfloat16)
    gate = jax.nn.sigmoid(jnp.dot(normed, w_gate, preferred_element_type=jnp.float32)).reshape(
        rows_here, cols_here, chans
    )
    factor = 2 if row_count == 4 * col_count else 1
    square_rows = factor * rows_here
    wide_rows = lax.all_gather(a_tile, "col", axis=1, tiled=True)
    spread = wide_rows.reshape(rows_here, row_count // factor, 1, square_rows, hidden)
    spread = jnp.repeat(spread, factor, axis=2).reshape(rows_here, row_count * square_rows, hidden)
    a_square = lax.all_to_all(spread, "row", split_axis=1, concat_axis=0, tiled=True)
    copies = jnp.tile(b_tile, (1, row_count // factor, 1))
    b_square = lax.all_to_all(copies, "row", split_axis=1, concat_axis=0, tiled=True)
    tri_square = jnp.einsum("kic,kjc->ijc", a_square, b_square, preferred_element_type=jnp.float32)
    normed_square = layer_norm(tri_square, ln_out_gain).astype(jnp.bfloat16)
    if factor == 1:
        tri_norm = normed_square
    else:
        parity = row_index % 2
        own_part = lax.dynamic_slice_in_dim(normed_square, parity * rows_here, rows_here, 0)
        other_part = lax.dynamic_slice_in_dim(normed_square, (1 - parity) * rows_here, rows_here, 0)
        received = swapped(other_part, "row", 0)
        tri_norm = jnp.where(
            parity == 0,
            jnp.concatenate([own_part, received], axis=1),
            jnp.concatenate([received, own_part], axis=1),
        )
    flat_norm = tri_norm.reshape(rows_here * cols_here, hidden)
    projected = jnp.dot(flat_norm, w_out, preferred_element_type=jnp.float32).reshape(
        rows_here, cols_here, chans
    )
    return (gate * projected).astype(jnp.bfloat16).reshape(rows_here, cols_here * chans)


def solution(mesh):
    in_specs = (P(("groups", "row"), "col"), P("groups"), P("groups"), P(), P(), P(), P(), P())
    out_specs = P(("groups", "row"), "col")
    return jax.shard_map(local, mesh=mesh, in_specs=in_specs, out_specs=out_specs, check_vma=False)
```
